32 devices in a mesh: row: 4 (over y, x), col: 8 (over z, core).
Axes of the slice: x: 2, y: 2, z: 4, core: 2. Of those that a mesh axis runs over, the one named last changes fastest.
Arguments:
- frame: bfloat16 [128, 256, 256], P('row', 'col'), may hold values from -6 to 6
- gain_attn: float32 [2, 256], replicated, may hold values from 0.1 to 1.9
- w_qkv: bfloat16 [2, 256, 768], replicated, may hold values from -2 to 2
- w_out: bfloat16 [2, 256, 256], replicated, may hold values from -1 to 1
- gain_mlp: float32 [2, 256], replicated, may hold values from 0.1 to 1.9
- w_up: bfloat16 [2, 256, 1024], replicated, may hold values from -0.375 to 0.375
- w_down: bfloat16 [2, 1024, 256], replicated, may hold values from -0.1875 to 0.1875
Outputs:
- result: bfloat16 [128, 256, 256], P('row', 'col')
The draws below stay inside these ranges and needn't reach their ends.
All inputs are finite; a program needn't handle non-finite values.
Results may differ from the reference program's by a relative error of at most 0.014.
The reference program's roundings to bfloat16 on the way count: a program that leaves them out, or rounds other values in their place, can miss the bound.
Values may be sent and summed in bfloat16 or wider, within the bound.
A program may use at most 128 MiB of HBM per device.

```python
import jax
import jax.numpy as jnp
from jax import lax

D = 256
HEADS = 8
FF = 1024
SW = 8
LAYERS = 2
HI = 128
WI = 256


def draw_w_qkv(key, part):
    base = jax.random.fold_in(key, 11)
    key_q, key_k, key_v = jax.random.split(base, 3)
    head_dim = D // HEADS
    shape = (LAYERS, D, HEADS, head_dim)
    query = jax.random.normal(key_q, shape, jnp.float32) * 1.6 * D ** (-0.5)
    keys = jax.random.normal(key_k, shape, jnp.float32) * 1.6 * D ** (-0.5)
    values = jax.random.normal(key_v, shape, jnp.float32) * D ** (-0.5)
    whole = jnp.concatenate([query.reshape(LAYERS, D, D), keys.reshape(LAYERS, D, D), values.reshape(LAYERS, D, D)], axis=-1)
    return jnp.clip(whole, -2.0, 2.0).astype(jnp.bfloat16)


def level_of(stream_key, dims, shards, smallest, largest):
    factor_of = 1.0
    for dim, shards_of in shards:
        draws = jax.random.uniform(jax.random.fold_in(jax.random.fold_in(stream_key, 6), dim), (shards_of,), jnp.float32, smallest / len(shards), largest / len(shards))
        factor_of = factor_of * jnp.repeat(jnp.exp(draws), dims[dim] // shards_of).reshape((-1,) + (1,) * (len(dims) - 1 - dim))
    return factor_of


def gaussian(stream_key, dims, scale, reach, cuts=(), held_as=jnp.bfloat16):
    level = level_of(stream_key, dims, cuts, -0.22, 0.18) if cuts else 1.0
    values = jax.random.normal(stream_key, dims, jnp.float32) * scale * level
    return jnp.minimum(jnp.maximum(values, -reach), reach).astype(held_as)


def setup_inputs(seed: int = 0) -> dict:
    arg_keys = jax.random.split(jax.random.key(seed), 8)
    return {
        "frame": gaussian(arg_keys[0], (HI, WI, D), 1.0, 6.0, ((0, 4), (1, 8))),
        "gain_attn": jnp.clip(1.0 + 0.18 * jax.random.normal(arg_keys[1], (LAYERS, D), jnp.float32), 0.1, 1.9),
        "w_qkv": draw_w_qkv(jax.random.fold_in(arg_keys[7], 71), 0),
        "w_out": gaussian(arg_keys[3], (LAYERS, D, D), (D // 8) ** -0.5, 1.0),
        "gain_mlp": jnp.clip(1.0 + 0.18 * jax.random.normal(arg_keys[4], (LAYERS, D), jnp.float32), 0.1, 1.9),
        "w_up": gaussian(arg_keys[5], (LAYERS, D, FF), D ** -0.5, 0.375),
        "w_down": gaussian(arg_keys[6], (LAYERS, FF, D), FF ** -0.5, 0.1875),
    }


EPS = 1e-05

def normalize(values, gain):
    floats = values.astype(jnp.float32)
    center = floats - lax.optimization_barrier(jnp.mean(floats, axis=-1, keepdims=True))
    spread = lax.optimization_barrier(jnp.mean(center * center, axis=-1, keepdims=True))
    return (center * lax.rsqrt(spread + EPS) * gain).astype(jnp.bfloat16)

def fdot(left, right):
    return jnp.dot(left.astype(jnp.float32), right.astype(jnp.float32), precision=lax.Precision.HIGHEST)

def attend(query, keys, values):
    length = query.shape[0]
    block = 512 if length % 512 == 0 else length
    factor = query.shape[1] ** (-0.5)
    blocks = query.reshape(length // block, block, query.shape[1])

    def single(rows):
        scores = fdot(rows, keys.T) * factor
        top = lax.optimization_barrier(jnp.max(scores, axis=-1, keepdims=True))
        probs = jnp.exp(scores - top)
        total = lax.optimization_barrier(jnp.sum(probs, axis=-1, keepdims=True))
        weights = lax.optimization_barrier(probs.astype(jnp.bfloat16))
        return (fdot(weights, values) / total).astype(jnp.bfloat16)
    return lax.map(single, blocks).reshape(length, query.shape[1])

def stripes(query, keys, values):
    return lax.map(lambda group: attend(group[0], group[1], group[2]), (query, keys, values))

def reference(frame, gain_attn, w_qkv, w_out, gain_mlp, w_up, w_down):
    head_dim = D // HEADS
    half = HEADS // 2
    height, width = (frame.shape[0], frame.shape[1])
    state = frame
    for layer in range(LAYERS):
        normed = normalize(state, gain_attn[layer])
        qkv = fdot(normed.reshape(-1, D), w_qkv[layer]).astype(jnp.bfloat16).reshape(height, width, 3 * D)
        parts = [qkv[:, :, index * D:(index + 1) * D] for index in range(3)]

        def horizontal(array):
            piece = array[:, :, :half * head_dim].reshape(height // SW, SW, width, half, head_dim)
            return piece.transpose(0, 3, 1, 2, 4).reshape(-1, SW * width, head_dim)

        def vertical(array):
            piece = array[:, :, half * head_dim:].reshape(height, width // SW, SW, half, head_dim)
            return piece.transpose(1, 3, 0, 2, 4).reshape(-1, height * SW, head_dim)
        across = stripes(*[horizontal(array) for array in parts])
        across = across.reshape(height // SW, half, SW, width, head_dim).transpose(0, 2, 3, 1, 4)
        across = across.reshape(height, width, half * head_dim)
        down = stripes(*[vertical(array) for array in parts])
        down = down.reshape(width // SW, half, height, SW, head_dim).transpose(2, 0, 3, 1, 4)
        down = down.reshape(height, width, half * head_dim)
        heads = jnp.concatenate([across, down], axis=-1).reshape(-1, D)
        mixed = state.reshape(-1, D).astype(jnp.float32) + fdot(heads, w_out[layer])
        normed2 = normalize(mixed, gain_mlp[layer])
        hidden = jax.nn.gelu(fdot(normed2, w_up[layer]), approximate=True).astype(jnp.bfloat16)
        state = (mixed + fdot(hidden, w_down[layer])).astype(jnp.bfloat16).reshape(height, width, D)
    return state
```

```python
import functools
import math

import jax
import jax.numpy as jnp
from jax import lax
from jax.experimental import pallas as pl
from jax.experimental.pallas import tpu as pltpu
from jax.sharding import PartitionSpec as P

D = 256
HEADS = 8
SW = 8
LAYERS = 2
HALF = HEADS // 2
HD = D // HEADS
EPS = 1e-05
SCALE = HD**-0.5 * math.log2(math.e)
REACH = 96.0
ONES = 16


def normalize(floats, gain):
    center = floats - jnp.mean(floats, axis=-1, keepdims=True)
    spread = jnp.mean(center * center, axis=-1, keepdims=True)
    return center * lax.rsqrt(spread + EPS) * gain


def project(normed, wt_ref, sent_a, sent_d):
    rows, bands, _, _ = normed.shape
    for band in range(rows // SW):
        tokens = normed[band * SW : (band + 1) * SW].reshape(-1, D).astype(jnp.bfloat16)
        qkv = lax.dot_general(
            wt_ref[: HALF * 3 * HD], tokens, (((1,), (1,)), ((), ())), preferred_element_type=jnp.float32
        ).astype(jnp.bfloat16)
        sent_a[band * HALF : (band + 1) * HALF] = qkv.reshape(HALF, 3 * HD, -1)
    for band in range(bands):
        tokens = normed[:, band].reshape(-1, D).astype(jnp.bfloat16)
        qkv = lax.dot_general(
            wt_ref[HALF * 3 * HD :], tokens, (((1,), (1,)), ((), ())), preferred_element_type=jnp.float32
        ).astype(jnp.bfloat16)
        sent_d[band * HALF : (band + 1) * HALF] = qkv.reshape(HALF, 3 * HD, -1)


def first_kernel(x_ref, gain_ref, wt_ref, sent_a, sent_d, normed):
    rows, cols, _ = x_ref.shape
    for band in range(rows // SW):
        part = slice(band * SW, (band + 1) * SW)
        floats = x_ref[part].reshape(-1, D).astype(jnp.float32)
        normed[part] = normalize(floats, gain_ref[...]).reshape(SW, cols // SW, SW, D)
    project(normed, wt_ref, sent_a, sent_d)


def rest(x_ref, heads_a, heads_d, w_out, gain_mlp, w_up, w_down, y_ref, mixed, normed, gain):
    rows, cols, _ = x_ref.shape
    bands = cols // SW
    flip = (((0,), (0,)), ((), ()))
    for band in range(bands):
        heads = heads_d[band * HALF : (band + 1) * HALF].reshape(HALF * HD, -1)
        part = lax.dot_general(heads, w_out[HALF * HD :], flip, preferred_element_type=jnp.float32)
        mixed[:, band] = part.reshape(rows, SW, D)
    for band in range(rows // SW):
        here = slice(band * SW, (band + 1) * SW)
        heads = heads_a[band * HALF : (band + 1) * HALF].reshape(HALF * HD, -1)
        part = lax.dot_general(heads, w_out[: HALF * HD], flip, preferred_element_type=jnp.float32)
        total = x_ref[here].reshape(-1, D).astype(jnp.float32) + (part + mixed[here].reshape(-1, D))
        normed2 = normalize(total, gain_mlp[...]).astype(jnp.bfloat16)
        up = jnp.dot(normed2, w_up[...], preferred_element_type=jnp.float32)
        hidden = jax.nn.gelu(up, approximate=True).astype(jnp.bfloat16)
        final = total + jnp.dot(hidden, w_down[...], preferred_element_type=jnp.float32)
        final = final.astype(jnp.bfloat16)
        y_ref[here] = final.reshape(SW, cols, D)
        if normed is not None:
            normed[here] = normalize(final.astype(jnp.float32), gain[...]).reshape(SW, bands, SW, D)


def middle_kernel(
    x_ref, heads_a, heads_d, w_out, gain_mlp, w_up, w_down, gain, wt_ref, y_ref, sent_a, sent_d, mixed, normed
):
    rest(x_ref, heads_a, heads_d, w_out, gain_mlp, w_up, w_down, y_ref, mixed, normed, gain)
    project(normed, wt_ref, sent_a, sent_d)


def last_kernel(x_ref, heads_a, heads_d, w_out, gain_mlp, w_up, w_down, y_ref, mixed):
    rest(x_ref, heads_a, heads_d, w_out, gain_mlp, w_up, w_down, y_ref, mixed, None, None)


def attend_kernel(got_ref, out_ref, keys, vals, queries):
    sources, items, _, width = got_ref.shape

    @pl.loop(0, items)
    def _(item):
        top_q = jnp.zeros((1, width), jnp.float32)
        top_k = jnp.zeros((1, width), jnp.float32)
        for src in range(sources):
            q = got_ref[src, item, :HD].astype(jnp.float32) * SCALE
            high = q.astype(jnp.bfloat16)
            low = (q - high.astype(jnp.float32)).astype(jnp.bfloat16)
            queries[src] = jnp.concatenate([high, low], axis=0)
            k = got_ref[src, item, HD : 2 * HD]
            keys[src * width : (src + 1) * width] = jnp.concatenate([k, k], axis=0).T
            kf = k.astype(jnp.float32)
            vals[src, :HD] = got_ref[src, item, 2 * HD :]
            vals[src, HD:] = jnp.ones((ONES, width), jnp.bfloat16)
            top_q = jnp.maximum(top_q, jnp.sum(q * q, axis=0, keepdims=True))
            top_k = jnp.maximum(top_k, jnp.sum(kf * kf, axis=0, keepdims=True))
        reach = jnp.max(top_q) * jnp.max(top_k)
        narrow = reach < REACH * REACH

        def scores(src, q):
            return jnp.dot(keys[src * width : (src + 1) * width], q, preferred_element_type=jnp.float32)

        def store(block, total):
            out_ref[block, item] = (total[:HD] / total[HD : HD + 1]).astype(jnp.bfloat16)

        @pl.when(narrow)
        def _():
            @pl.loop(0, sources)
            def _(block):
                q = queries[block]
                total = jnp.zeros((HD + ONES, width), jnp.float32)
                for src in range(sources):
                    probs = jnp.exp2(scores(src, q)).astype(jnp.bfloat16)
                    total += jnp.dot(vals[src], probs, preferred_element_type=jnp.float32)
                store(block, total)

        @pl.when(jnp.logical_not(narrow))
        def _():
            @pl.loop(0, sources)
            def _(block):
                q = queries[block]
                top = jnp.full((1, width), -jnp.inf, jnp.float32)
                for src in range(sources):
                    top = jnp.maximum(top, jnp.max(scores(src, q), axis=0, keepdims=True))
                total = jnp.zeros((HD + ONES, width), jnp.float32)
                for src in range(sources):
                    probs = jnp.exp2(scores(src, q) - top).astype(jnp.bfloat16)
                    total += jnp.dot(vals[src], probs, preferred_element_type=jnp.float32)
                store(block, total)


VM = pl.BlockSpec(memory_space=pltpu.VMEM)


def call(kernel, outs, scratch, *args):
    return pl.pallas_call(
        kernel,
        out_shape=outs,
        in_specs=[VM] * len(args),
        out_specs=jax.tree.map(lambda _: VM, outs),
        scratch_shapes=scratch,
    )(*args)


def attend(got):
    sources, items, _, width = got.shape
    return call(
        attend_kernel,
        jax.ShapeDtypeStruct((sources, items, HD, width), jnp.bfloat16),
        [
            pltpu.VMEM((sources * width, 2 * HD), jnp.bfloat16),
            pltpu.VMEM((sources, HD + ONES, width), jnp.bfloat16),
            pltpu.VMEM((sources, 2 * HD, width), jnp.bfloat16),
        ],
        got,
    )


def exchange(array, axis):
    count = lax.axis_size(axis)
    split = array.reshape(count, -1, *array.shape[-2:])
    return lax.all_to_all(split, axis, split_axis=0, concat_axis=0, tiled=True)


def shards(frame, gain_attn, w_qkv, w_out, gain_mlp, w_up, w_down):
    rows, cols, _ = frame.shape
    items_a = rows // SW * HALF
    items_d = cols // SW * HALF
    wt = w_qkv.reshape(LAYERS, D, 3, HEADS, HD).transpose(0, 3, 2, 4, 1).reshape(LAYERS, 3 * D, D)
    sent = (
        jax.ShapeDtypeStruct((items_a, 3 * HD, SW * cols), jnp.bfloat16),
        jax.ShapeDtypeStruct((items_d, 3 * HD, SW * rows), jnp.bfloat16),
    )
    scratch = pltpu.VMEM((rows, cols // SW, SW, D), jnp.float32)
    shape = jax.ShapeDtypeStruct(frame.shape, jnp.bfloat16)
    state = frame
    sent_a, sent_d = call(first_kernel, sent, [scratch], frame, gain_attn[:1], wt[0])
    for layer in range(LAYERS):
        heads_d = exchange(attend(exchange(sent_d, "row")), "row").reshape(items_d, HD, -1)
        heads_a = exchange(attend(exchange(sent_a, "col")), "col").reshape(items_a, HD, -1)
        args = (state, heads_a, heads_d, w_out[layer], gain_mlp[layer : layer + 1], w_up[layer], w_down[layer])
        if layer + 1 < LAYERS:
            state, sent_a, sent_d = call(
                middle_kernel,
                (shape,) + sent,
                [scratch, scratch],
                *args,
                gain_attn[layer + 1 : layer + 2],
                wt[layer + 1],
            )
        else:
            state = call(last_kernel, shape, [scratch], *args)
    return state


def solution(mesh):
    placed = (P("row", "col", None), P(), P(), P(), P(), P(), P())
    return jax.shard_map(
        shards, mesh=mesh, in_specs=placed, out_specs=P("row", "col", None), check_vma=False
    )
```

```python
import functools
import math

import jax
import jax.numpy as jnp
from jax import lax
from jax.experimental import pallas as pl
from jax.experimental.pallas import tpu as pltpu
from jax.sharding import PartitionSpec as P

D = 256
HEADS = 8
SW = 8
LAYERS = 2
HALF = HEADS // 2
HD = D // HEADS
EPS = 1e-05
SCALE = HD**-0.5 * math.log2(math.e)


def normalize(floats, gain):
    center = floats - jnp.mean(floats, axis=-1, keepdims=True)
    spread = jnp.mean(center * center, axis=-1, keepdims=True)
    return center * lax.rsqrt(spread + EPS) * gain


def project(normed, w_ref, sent_a, sent_d, wt):
    rows, bands, _, _ = normed.shape
    side = HALF * HD
    for part in range(3):
        wt[part] = w_ref[:, part * D : (part + 1) * D].T

    def emit(tokens, first, sent, band):
        tokens = tokens.reshape(-1, D).astype(jnp.bfloat16)
        for part in range(3):
            out = lax.dot_general(
                wt[part, first : first + side],
                tokens,
                (((1,), (1,)), ((), ())),
                preferred_element_type=jnp.float32,
            )
            sent[band * HALF : (band + 1) * HALF, part * HD : (part + 1) * HD] = (
                out.astype(jnp.bfloat16).reshape(HALF, HD, -1)
            )

    for band in range(bands):
        emit(normed[:, band], side, sent_d, band)
    for band in range(rows // SW):
        emit(normed[band * SW : (band + 1) * SW], 0, sent_a, band)


def first_kernel(x_ref, gain_ref, w_ref, sent_a, sent_d, normed, wt):
    rows, cols, _ = x_ref.shape
    for band in range(rows // SW):
        part = slice(band * SW, (band + 1) * SW)
        floats = x_ref[part].reshape(-1, D).astype(jnp.float32)
        normed[part] = normalize(floats, gain_ref[...]).reshape(SW, cols // SW, SW, D)
    project(normed, w_ref, sent_a, sent_d, wt)


def rest(x_ref, heads_a, heads_d, w_out, gain_mlp, w_up, w_down, y_ref, mixed, normed, gain):
    rows, cols, _ = x_ref.shape
    bands = cols // SW
    flip = (((0,), (0,)), ((), ()))
    for band in range(bands):
        heads = heads_d[band * HALF : (band + 1) * HALF].reshape(HALF * HD, -1)
        part = lax.dot_general(heads, w_out[HALF * HD :], flip, preferred_element_type=jnp.float32)
        mixed[:, band] = part.reshape(rows, SW, D)
    for band in range(rows // SW):
        here = slice(band * SW, (band + 1) * SW)
        heads = heads_a[band * HALF : (band + 1) * HALF].reshape(HALF * HD, -1)
        part = lax.dot_general(heads, w_out[: HALF * HD], flip, preferred_element_type=jnp.float32)
        total = x_ref[here].reshape(-1, D).astype(jnp.float32) + (part + mixed[here].reshape(-1, D))
        normed2 = normalize(total, gain_mlp[...]).astype(jnp.bfloat16)
        up = jnp.dot(normed2, w_up[...], preferred_element_type=jnp.float32)
        hidden = jax.nn.gelu(up, approximate=True).astype(jnp.bfloat16)
        final = total + jnp.dot(hidden, w_down[...], preferred_element_type=jnp.float32)
        final = final.astype(jnp.bfloat16)
        y_ref[here] = final.reshape(SW, cols, D)
        if normed is not None:
            normed[here] = normalize(final.astype(jnp.float32), gain[...]).reshape(SW, bands, SW, D)


def middle_kernel(
    x_ref, heads_a, heads_d, w_out, gain_mlp, w_up, w_down, gain, w_ref, y_ref, sent_a, sent_d, mixed, normed, wt
):
    rest(x_ref, heads_a, heads_d, w_out, gain_mlp, w_up, w_down, y_ref, mixed, normed, gain)
    project(normed, w_ref, sent_a, sent_d, wt)


def last_kernel(x_ref, heads_a, heads_d, w_out, gain_mlp, w_up, w_down, y_ref, mixed):
    rest(x_ref, heads_a, heads_d, w_out, gain_mlp, w_up, w_down, y_ref, mixed, None, None)


def wrap(index, count):
    return lax.rem(index + count, count)


class Stream:
    def __init__(self, axis, sent, heads, got, outs, keys, vals, queries, board, tops, sems):
        self.axis, self.sent, self.heads, self.got, self.outs = axis, sent, heads, got, outs
        self.keys, self.vals, self.queries, self.board, self.tops = keys, vals, queries, board, tops
        self.send_in, self.recv_in, self.send_out, self.recv_out, self.local = sems
        self.count, self.items, _, self.width = got.shape
        self.me = lax.axis_index(axis)
        self.units = self.count * self.items

    def greet(self, barrier):
        for step in range(1, self.count):
            pl.semaphore_signal(barrier, inc=1, device_id={self.axis: wrap(self.me + step, self.count)})

    def inward(self, item, step):
        target = wrap(self.me + step, self.count)
        return pltpu.make_async_remote_copy(
            src_ref=self.sent.at[target, item],
            dst_ref=self.got.at[step, item],
            send_sem=self.send_in.at[item, step],
            recv_sem=self.recv_in.at[item, step],
            device_id={self.axis: target},
        )

    def outward(self, item, step):
        return pltpu.make_async_remote_copy(
            src_ref=self.outs.at[step, item],
            dst_ref=self.heads.at[self.me, item],
            send_sem=self.send_out.at[item, step],
            recv_sem=self.recv_out.at[item, step],
            device_id={self.axis: wrap(self.me - step, self.count)},
        )

    def own(self):
        return pltpu.make_async_copy(self.sent.at[self.me], self.got.at[0], self.local)

    def start(self, item):
        for step in range(1, self.count):
            self.inward(item, step).start()

    def prepare(self, item):
        for step in range(1, self.count):
            self.inward(item, step).wait_recv()
        slot = lax.rem(item, 2)
        for src in range(self.count):
            q = self.got[src, item, :HD].astype(jnp.float32) * SCALE
            high = q.astype(jnp.bfloat16)
            low = (q - high.astype(jnp.float32)).astype(jnp.bfloat16)
            self.queries[src] = jnp.concatenate([high, low], axis=0)
            k = self.got[src, item, HD : 2 * HD]
            self.keys[src * self.width : (src + 1) * self.width] = jnp.concatenate([k, k], axis=0).T
            self.vals[slot, src] = self.got[src, item, 2 * HD :]

    def score(self, unit):
        slot = lax.rem(unit, 2)
        q = self.queries[lax.rem(unit, self.count)]
        tops = []
        for src in range(self.count):
            here = slice(src * self.width, (src + 1) * self.width)
            scores = jnp.dot(self.keys[here], q, preferred_element_type=jnp.float32)
            self.board[slot, here] = scores
            tops.append(jnp.max(scores.reshape(-1, 8, self.width), axis=0))
        self.tops[slot] = jnp.max(functools.reduce(jnp.maximum, tops), axis=0, keepdims=True)

    def finish(self, unit):
        slot = lax.rem(unit, 2)
        item, block = unit // self.count, lax.rem(unit, self.count)
        top = self.tops[slot]
        sums, total = 0.0, 0.0
        for src in range(self.count):
            here = slice(src * self.width, (src + 1) * self.width)
            probs = jnp.exp2(self.board[slot, here] - top)
            sums += jnp.sum(probs.reshape(-1, 8, self.width), axis=0)
            total += jnp.dot(
                self.vals[lax.rem(item, 2), src], probs.astype(jnp.bfloat16), preferred_element_type=jnp.float32
            )
        result = (total / jnp.sum(sums, axis=0, keepdims=True)).astype(jnp.bfloat16)
        self.outs[block, item] = result

    def deliver(self, unit):
        item, block = unit // self.count, lax.rem(unit, self.count)

        @pl.when(block == 0)
        def _():
            self.heads[self.me, item] = self.outs[0, item]

        @pl.when(block != 0)
        def _():
            self.outward(item, block).start()

    def run(self):
        self.prepare(0)
        self.score(0)

        @pl.loop(0, self.units - 1)
        def _(unit):
            after = unit + 1

            @pl.when(lax.rem(after, self.count) == 0)
            def _():
                self.prepare(after // self.count)

            self.score(after)
            self.finish(unit)

            @pl.when(unit > 0)
            def _():
                self.deliver(unit - 1)

        self.finish(self.units - 1)
        if self.units > 1:
            self.deliver(self.units - 2)
        self.deliver(self.units - 1)

    def drain(self):
        for item in range(self.items):
            for step in range(1, self.count):
                self.inward(item, step).wait_send()
                self.outward(item, step).wait()


def layer_kernel(
    sent_a, sent_d, heads_a, heads_d, got_a, got_d, outs_a, outs_d, keys, vals, queries, board, tops, *sems
):
    def stream(axis, sent, heads, got, outs, sems):
        count, _, _, width = got.shape
        return Stream(
            axis,
            sent,
            heads,
            got,
            outs,
            keys.at[: count * width],
            vals.at[:, :count],
            queries.at[:count],
            board.at[:, : count * width],
            tops,
            sems,
        )

    across = stream("col", sent_a, heads_a, got_a, outs_a, sems[:5])
    down = stream("row", sent_d, heads_d, got_d, outs_d, sems[5:])
    barrier = pltpu.get_barrier_semaphore()
    across.greet(barrier)
    down.greet(barrier)
    pl.semaphore_wait(barrier, across.count + down.count - 2)
    for item in range(down.items):
        down.start(item)
        if item == 0:
            across.start(item)
    for item in range(1, across.items):
        across.start(item)
    across.own().start()
    down.own().start()
    across.own().wait()
    down.own().wait()
    down.run()
    across.run()
    down.drain()
    across.drain()


VM = pl.BlockSpec(memory_space=pltpu.VMEM)


def call(kernel, outs, scratch, *args, params=None):
    def spec(arg):
        if not isinstance(arg, tuple):
            return VM
        array, layer = arg
        rest = array.shape[1:]
        return pl.BlockSpec((None,) + rest, lambda i: (layer,) + (0,) * len(rest))

    return pl.pallas_call(
        kernel,
        out_shape=outs,
        grid=(1,),
        in_specs=[spec(arg) for arg in args],
        out_specs=jax.tree.map(lambda _: VM, outs),
        scratch_shapes=scratch,
        compiler_params=params,
    )(*[arg[0] if isinstance(arg, tuple) else arg for arg in args])


def split(array, axis):
    return array.reshape(lax.axis_size(axis), -1, *array.shape[-2:])


def attend(sent_a, sent_d, layer):
    sent_a, sent_d = split(sent_a, "col"), split(sent_d, "row")
    scratch, sems, outs = [], [], []
    for sent in (sent_a, sent_d):
        count, items, _, width = sent.shape
        outs.append(jax.ShapeDtypeStruct((count, items, HD, width), jnp.bfloat16))
        scratch.append(pltpu.VMEM(sent.shape, jnp.bfloat16))
        sems += [pltpu.SemaphoreType.DMA((items, count))] * 4 + [pltpu.SemaphoreType.DMA]
    for out in outs:
        scratch.append(pltpu.VMEM(out.shape, jnp.bfloat16))
    count = max(sent_a.shape[0], sent_d.shape[0])
    width = max(sent_a.shape[-1], sent_d.shape[-1])
    scratch += [
        pltpu.VMEM((count * width, 2 * HD), jnp.bfloat16),
        pltpu.VMEM((2, count, HD, width), jnp.bfloat16),
        pltpu.VMEM((count, 2 * HD, width), jnp.bfloat16),
        pltpu.VMEM((2, count * width, width), jnp.float32),
        pltpu.VMEM((2, 1, width), jnp.float32),
    ]
    heads = call(
        layer_kernel,
        tuple(outs),
        scratch + sems,
        sent_a,
        sent_d,
        params=pltpu.CompilerParams(collective_id=layer, has_side_effects=True),
    )
    return [array.reshape(-1, *array.shape[-2:]) for array in heads]


def shards(frame, gain_attn, w_qkv, w_out, gain_mlp, w_up, w_down):
    rows, cols, _ = frame.shape
    items_a = rows // SW * HALF
    items_d = cols // SW * HALF
    gain_attn, gain_mlp = gain_attn[:, None], gain_mlp[:, None]
    sent = (
        jax.ShapeDtypeStruct((items_a, 3 * HD, SW * cols), jnp.bfloat16),
        jax.ShapeDtypeStruct((items_d, 3 * HD, SW * rows), jnp.bfloat16),
    )
    tokens = pltpu.VMEM((rows, cols // SW, SW, D), jnp.float32)
    flipped = pltpu.VMEM((3, D, D), jnp.bfloat16)
    shape = jax.ShapeDtypeStruct(frame.shape, jnp.bfloat16)
    state = frame
    sent_a, sent_d = call(first_kernel, sent, [tokens, flipped], frame, (gain_attn, 0), (w_qkv, 0))
    for layer in range(LAYERS):
        heads_a, heads_d = attend(sent_a, sent_d, layer)
        args = (state, heads_a, heads_d, *[(array, layer) for array in (w_out, gain_mlp, w_up, w_down)])
        if layer + 1 < LAYERS:
            state, sent_a, sent_d = call(
                middle_kernel,
                (shape,) + sent,
                [tokens, tokens, flipped],
                *args,
                (gain_attn, layer + 1),
                (w_qkv, layer + 1),
            )
        else:
            state = call(last_kernel, shape, [tokens], *args)
    return state


def solution(mesh):
    placed = (P("row", "col", None), P(), P(), P(), P(), P(), P())
    return jax.shard_map(
        shards, mesh=mesh, in_specs=placed, out_specs=P("row", "col", None), check_vma=False
    )
```

```python
import functools
import math

import jax
import jax.numpy as jnp
from jax import lax
from jax.experimental import pallas as pl
from jax.experimental.pallas import tpu as pltpu
from jax.sharding import PartitionSpec as P

D = 256
HEADS = 8
SW = 8
LAYERS = 2
HALF = HEADS // 2
HD = D // HEADS
EPS = 1e-05
SCALE = HD**-0.5 * math.log2(math.e)


def normalize(floats, gain):
    center = floats - jnp.mean(floats, axis=-1, keepdims=True)
    spread = jnp.mean(center * center, axis=-1, keepdims=True)
    return center * lax.rsqrt(spread + EPS) * gain


def project(normed, w_ref, sent_a, sent_d, wt):
    rows, bands, _, _ = normed.shape
    side = HALF * HD
    for part in range(3):
        wt[part] = w_ref[:, part * D : (part + 1) * D].T

    def emit(tokens, first, sent, band):
        tokens = tokens.reshape(-1, D).astype(jnp.bfloat16)
        for part in range(3):
            out = lax.dot_general(
                wt[part, first : first + side],
                tokens,
                (((1,), (1,)), ((), ())),
                preferred_element_type=jnp.float32,
            )
            sent[band * HALF : (band + 1) * HALF, part * HD : (part + 1) * HD] = (
                out.astype(jnp.bfloat16).reshape(HALF, HD, -1)
            )

    for band in range(bands):
        emit(normed[:, band], side, sent_d, band)
    for band in range(rows // SW):
        emit(normed[band * SW : (band + 1) * SW], 0, sent_a, band)


def first_kernel(layer, x_ref, gain_ref, w_ref, sent_a, sent_d, normed, wt):
    rows, cols, _ = x_ref.shape
    for band in range(rows // SW):
        part = slice(band * SW, (band + 1) * SW)
        floats = x_ref[part].reshape(-1, D).astype(jnp.float32)
        normed[part] = normalize(floats, gain_ref[layer : layer + 1]).reshape(SW, cols // SW, SW, D)
    project(normed, w_ref, sent_a, sent_d, wt)


def rest(layer, x_ref, heads_a, heads_d, w_out, gain_mlp, w_up, w_down, y_ref, mixed, normed, gain):
    rows, cols, _ = x_ref.shape
    bands = cols // SW
    flip = (((0,), (0,)), ((), ()))
    for band in range(bands):
        heads = heads_d[band * HALF : (band + 1) * HALF].reshape(HALF * HD, -1)
        part = lax.dot_general(heads, w_out[HALF * HD :], flip, preferred_element_type=jnp.float32)
        mixed[:, band] = part.reshape(rows, SW, D)
    for band in range(rows // SW):
        here = slice(band * SW, (band + 1) * SW)
        heads = heads_a[band * HALF : (band + 1) * HALF].reshape(HALF * HD, -1)
        part = lax.dot_general(heads, w_out[: HALF * HD], flip, preferred_element_type=jnp.float32)
        total = x_ref[here].reshape(-1, D).astype(jnp.float32) + (part + mixed[here].reshape(-1, D))
        normed2 = normalize(total, gain_mlp[layer : layer + 1]).astype(jnp.bfloat16)
        up = jnp.dot(normed2, w_up[...], preferred_element_type=jnp.float32)
        hidden = jax.nn.gelu(up, approximate=True).astype(jnp.bfloat16)
        final = total + jnp.dot(hidden, w_down[...], preferred_element_type=jnp.float32)
        final = final.astype(jnp.bfloat16)
        y_ref[here] = final.reshape(SW, cols, D)
        if normed is not None:
            normed[here] = normalize(final.astype(jnp.float32), gain[layer + 1 : layer + 2]).reshape(SW, bands, SW, D)


def middle_kernel(
    layer, x_ref, heads_a, heads_d, w_out, gain_mlp, w_up, w_down, gain, w_ref, y_ref, sent_a, sent_d, mixed, normed, wt
):
    rest(layer, x_ref, heads_a, heads_d, w_out, gain_mlp, w_up, w_down, y_ref, mixed, normed, gain)
    project(normed, w_ref, sent_a, sent_d, wt)


def last_kernel(layer, x_ref, heads_a, heads_d, w_out, gain_mlp, w_up, w_down, y_ref, mixed):
    rest(layer, x_ref, heads_a, heads_d, w_out, gain_mlp, w_up, w_down, y_ref, mixed, None, None)


def wrap(index, count):
    return lax.rem(index + count, count)


class Stream:
    def __init__(self, axis, sent, heads, got, outs, keys, vals, queries, board, tops, sems):
        self.axis, self.sent, self.heads, self.got, self.outs = axis, sent, heads, got, outs
        self.keys, self.vals, self.queries, self.board, self.tops = keys, vals, queries, board, tops
        self.send_in, self.recv_in, self.send_out, self.recv_out, self.local = sems
        self.count, self.items, _, self.width = got.shape
        self.me = lax.axis_index(axis)
        self.units = self.count * self.items

    def greet(self, barrier):
        for step in range(1, self.count):
            pl.semaphore_signal(barrier, inc=1, device_id={self.axis: wrap(self.me + step, self.count)})

    def inward(self, item, step):
        target = wrap(self.me + step, self.count)
        return pltpu.make_async_remote_copy(
            src_ref=self.sent.at[target, item],
            dst_ref=self.got.at[step, item],
            send_sem=self.send_in.at[item, step],
            recv_sem=self.recv_in.at[item, step],
            device_id={self.axis: target},
        )

    def outward(self, item, step):
        return pltpu.make_async_remote_copy(
            src_ref=self.outs.at[step, item],
            dst_ref=self.heads.at[self.me, item],
            send_sem=self.send_out.at[item, step],
            recv_sem=self.recv_out.at[item, step],
            device_id={self.axis: wrap(self.me - step, self.count)},
        )

    def own(self):
        return pltpu.make_async_copy(self.sent.at[self.me], self.got.at[0], self.local)

    def start(self, item):
        for step in range(1, self.count):
            self.inward(item, step).start()

    def prepare(self, item):
        for step in range(1, self.count):
            self.inward(item, step).wait_recv()
        slot = lax.rem(item, 2)
        for src in range(self.count):
            q = self.got[src, item, :HD].astype(jnp.float32) * SCALE
            high = q.astype(jnp.bfloat16)
            low = (q - high.astype(jnp.float32)).astype(jnp.bfloat16)
            self.queries[src] = jnp.concatenate([high, low], axis=0)
            k = self.got[src, item, HD : 2 * HD]
            self.keys[src * self.width : (src + 1) * self.width] = jnp.concatenate([k, k], axis=0).T
            self.vals[slot, src] = self.got[src, item, 2 * HD :]

    def step(self, after, unit):
        count, width = self.count, self.width
        if after is not None:
            after, odd = after
            q = self.queries[lax.rem(after, count)]
            tops = []
        if unit is not None:
            unit, even = unit
            item, block = unit // count, lax.rem(unit, count)
            slot = lax.rem(item, 2)
            top = self.tops[even][...]
            sums, total = 0.0, 0.0
        for src in range(count):
            here = slice(src * width, (src + 1) * width)
            if after is not None:
                scores = jnp.dot(self.keys[here], q, preferred_element_type=jnp.float32)
                self.board[odd][here] = scores
                tops.append(jnp.max(scores.reshape(-1, 8, width), axis=0))
            if unit is not None:
                probs = jnp.exp2(self.board[even][here] - top)
                sums += jnp.sum(probs.reshape(-1, 8, width), axis=0)
                total += jnp.dot(
                    self.vals[slot, src], probs.astype(jnp.bfloat16), preferred_element_type=jnp.float32
                )
        if after is not None:
            self.tops[odd][...] = jnp.max(functools.reduce(jnp.maximum, tops), axis=0, keepdims=True)
        if unit is not None:
            self.outs[block, item] = (total / jnp.sum(sums, axis=0, keepdims=True)).astype(jnp.bfloat16)

    def deliver(self, unit):
        item, block = unit // self.count, lax.rem(unit, self.count)

        @pl.when(block == 0)
        def _():
            self.heads[self.me, item] = self.outs[0, item]

        @pl.when(block != 0)
        def _():
            self.outward(item, block).start()

    def run(self):
        units = self.units
        assert self.count % 2 == 0
        self.prepare(0)
        self.step((0, 0), None)

        @pl.loop(0, units - 2, step=2)
        def _(unit):
            self.step((unit + 1, 1), (unit, 0))

            @pl.when(unit > 0)
            def _():
                self.deliver(unit - 1)

            after = unit + 2

            @pl.when(lax.rem(after, self.count) == 0)
            def _():
                self.prepare(after // self.count)

            self.step((after, 0), (unit + 1, 1))
            self.deliver(unit)

        self.step((units - 1, 1), (units - 2, 0))
        if units > 2:
            self.deliver(units - 3)
        self.step(None, (units - 1, 1))
        self.deliver(units - 2)
        self.deliver(units - 1)

    def drain(self):
        for item in range(self.items):
            for step in range(1, self.count):
                self.inward(item, step).wait_send()
                self.outward(item, step).wait()


def layer_kernel(
    sent_a, sent_d, heads_a, heads_d, got_a, got_d, outs_a, outs_d, keys, vals, queries, even, odd, even_top, odd_top, *sems
):
    def stream(axis, sent, heads, got, outs, sems):
        count, _, _, width = got.shape
        return Stream(
            axis,
            sent,
            heads,
            got,
            outs,
            keys.at[: count * width],
            vals.at[:, :count],
            queries.at[:count],
            (even.at[: count * width], odd.at[: count * width]),
            (even_top, odd_top),
            sems,
        )

    across = stream("col", sent_a, heads_a, got_a, outs_a, sems[:5])
    down = stream("row", sent_d, heads_d, got_d, outs_d, sems[5:])
    barrier = pltpu.get_barrier_semaphore()
    across.greet(barrier)
    down.greet(barrier)
    pl.semaphore_wait(barrier, across.count + down.count - 2)
    for item in range(down.items):
        down.start(item)
        if item == 0:
            across.start(item)
    for item in range(1, across.items):
        across.start(item)
    across.own().start()
    down.own().start()
    across.own().wait()
    down.own().wait()
    down.run()
    across.run()
    down.drain()
    across.drain()


VM = pl.BlockSpec(memory_space=pltpu.VMEM)


def call(kernel, outs, scratch, *args, params=None):
    def spec(arg):
        if not isinstance(arg, tuple):
            return VM
        array, layer = arg
        rest = array.shape[1:]
        return pl.BlockSpec((None,) + rest, lambda i: (layer,) + (0,) * len(rest))

    return pl.pallas_call(
        kernel,
        out_shape=outs,
        grid=(1,),
        in_specs=[spec(arg) for arg in args],
        out_specs=jax.tree.map(lambda _: VM, outs),
        scratch_shapes=scratch,
        compiler_params=params,
    )(*[arg[0] if isinstance(arg, tuple) else arg for arg in args])


def split(array, axis):
    return array.reshape(lax.axis_size(axis), -1, *array.shape[-2:])


def attend(sent_a, sent_d, layer):
    sent_a, sent_d = split(sent_a, "col"), split(sent_d, "row")
    scratch, sems, outs = [], [], []
    for sent in (sent_a, sent_d):
        count, items, _, width = sent.shape
        outs.append(jax.ShapeDtypeStruct((count, items, HD, width), jnp.bfloat16))
        scratch.append(pltpu.VMEM(sent.shape, jnp.bfloat16))
        sems += [pltpu.SemaphoreType.DMA((items, count))] * 4 + [pltpu.SemaphoreType.DMA]
    for out in outs:
        scratch.append(pltpu.VMEM(out.shape, jnp.bfloat16))
    count = max(sent_a.shape[0], sent_d.shape[0])
    width = max(sent_a.shape[-1], sent_d.shape[-1])
    scratch += [
        pltpu.VMEM((count * width, 2 * HD), jnp.bfloat16),
        pltpu.VMEM((2, count, HD, width), jnp.bfloat16),
        pltpu.VMEM((count, 2 * HD, width), jnp.bfloat16),
        pltpu.VMEM((count * width, width), jnp.float32),
        pltpu.VMEM((count * width, width), jnp.float32),
        pltpu.VMEM((1, width), jnp.float32),
        pltpu.VMEM((1, width), jnp.float32),
    ]
    heads = call(
        layer_kernel,
        tuple(outs),
        scratch + sems,
        sent_a,
        sent_d,
        params=pltpu.CompilerParams(collective_id=layer, has_side_effects=True),
    )
    return [array.reshape(-1, *array.shape[-2:]) for array in heads]


def shards(frame, gain_attn, w_qkv, w_out, gain_mlp, w_up, w_down):
    rows, cols, _ = frame.shape
    items_a = rows // SW * HALF
    items_d = cols // SW * HALF
    sent = (
        jax.ShapeDtypeStruct((items_a, 3 * HD, SW * cols), jnp.bfloat16),
        jax.ShapeDtypeStruct((items_d, 3 * HD, SW * rows), jnp.bfloat16),
    )
    tokens = pltpu.VMEM((rows, cols // SW, SW, D), jnp.float32)
    flipped = pltpu.VMEM((3, D, D), jnp.bfloat16)
    shape = jax.ShapeDtypeStruct(frame.shape, jnp.bfloat16)
    state = frame
    sent_a, sent_d = call(functools.partial(first_kernel, 0), sent, [tokens, flipped], frame, gain_attn, (w_qkv, 0))
    for layer in range(LAYERS):
        heads_a, heads_d = attend(sent_a, sent_d, layer)
        args = (state, heads_a, heads_d, (w_out, layer), gain_mlp, (w_up, layer), (w_down, layer))
        if layer + 1 < LAYERS:
            state, sent_a, sent_d = call(
                functools.partial(middle_kernel, layer),
                (shape,) + sent,
                [tokens, tokens, flipped],
                *args,
                gain_attn,
                (w_qkv, layer + 1),
            )
        else:
            state = call(functools.partial(last_kernel, layer), shape, [tokens], *args)
    return state


def solution(mesh):
    placed = (P("row", "col", None), P(), P(), P(), P(), P(), P())
    return jax.shard_map(
        shards, mesh=mesh, in_specs=placed, out_specs=P("row", "col", None), check_vma=False
    )
```

```python
import functools
import math

import jax
import jax.numpy as jnp
from jax import lax
from jax.experimental import pallas as pl
from jax.experimental.pallas import tpu as pltpu
from jax.sharding import PartitionSpec as P

D = 256
HEADS = 8
SW = 8
LAYERS = 2
HALF = HEADS // 2
HD = D // HEADS
EPS = 1e-05
UNROLL = 4
LAG = 2
SCALE = HD**-0.5 * math.log2(math.e)


def normalize(floats, gain):
    center = floats - jnp.mean(floats, axis=-1, keepdims=True)
    spread = jnp.mean(center * center, axis=-1, keepdims=True)
    return center * lax.rsqrt(spread + EPS) * gain


def project(normed, w_ref, sent_a, sent_d, wt):
    rows, bands, _, _ = normed.shape
    side = HALF * HD
    for part in range(3):
        wt[part] = w_ref[:, part * D : (part + 1) * D].T

    def emit(tokens, first, sent, band):
        tokens = tokens.reshape(-1, D).astype(jnp.bfloat16)
        for part in range(3):
            out = lax.dot_general(
                wt[part, first : first + side],
                tokens,
                (((1,), (1,)), ((), ())),
                preferred_element_type=jnp.float32,
            )
            sent[band * HALF : (band + 1) * HALF, part * HD : (part + 1) * HD] = (
                out.astype(jnp.bfloat16).reshape(HALF, HD, -1)
            )

    for band in range(bands):
        emit(normed[:, band], side, sent_d, band)
    for band in range(rows // SW):
        emit(normed[band * SW : (band + 1) * SW], 0, sent_a, band)


def first_kernel(layer, x_ref, gain_ref, w_ref, sent_a, sent_d, normed, wt):
    rows, cols, _ = x_ref.shape
    for band in range(rows // SW):
        part = slice(band * SW, (band + 1) * SW)
        floats = x_ref[part].reshape(-1, D).astype(jnp.float32)
        normed[part] = normalize(floats, gain_ref[layer : layer + 1]).reshape(SW, cols // SW, SW, D)
    project(normed, w_ref, sent_a, sent_d, wt)


def rest(layer, x_ref, heads_a, heads_d, w_out, gain_mlp, w_up, w_down, y_ref, mixed, normed, gain):
    rows, cols, _ = x_ref.shape
    bands = cols // SW
    flip = (((0,), (0,)), ((), ()))
    for band in range(bands):
        heads = heads_d[band * HALF : (band + 1) * HALF].reshape(HALF * HD, -1)
        part = lax.dot_general(heads, w_out[HALF * HD :], flip, preferred_element_type=jnp.float32)
        mixed[:, band] = part.reshape(rows, SW, D)
    for band in range(rows // SW):
        here = slice(band * SW, (band + 1) * SW)
        heads = heads_a[band * HALF : (band + 1) * HALF].reshape(HALF * HD, -1)
        part = lax.dot_general(heads, w_out[: HALF * HD], flip, preferred_element_type=jnp.float32)
        total = x_ref[here].reshape(-1, D).astype(jnp.float32) + (part + mixed[here].reshape(-1, D))
        normed2 = normalize(total, gain_mlp[layer : layer + 1]).astype(jnp.bfloat16)
        up = jnp.dot(normed2, w_up[...], preferred_element_type=jnp.float32)
        hidden = jax.nn.gelu(up, approximate=True).astype(jnp.bfloat16)
        final = total + jnp.dot(hidden, w_down[...], preferred_element_type=jnp.float32)
        final = final.astype(jnp.bfloat16)
        y_ref[here] = final.reshape(SW, cols, D)
        if normed is not None:
            normed[here] = normalize(final.astype(jnp.float32), gain[layer + 1 : layer + 2]).reshape(SW, bands, SW, D)


def middle_kernel(
    layer, x_ref, heads_a, heads_d, w_out, gain_mlp, w_up, w_down, gain, w_ref, y_ref, sent_a, sent_d, mixed, normed, wt
):
    rest(layer, x_ref, heads_a, heads_d, w_out, gain_mlp, w_up, w_down, y_ref, mixed, normed, gain)
    project(normed, w_ref, sent_a, sent_d, wt)


def last_kernel(layer, x_ref, heads_a, heads_d, w_out, gain_mlp, w_up, w_down, y_ref, mixed):
    rest(layer, x_ref, heads_a, heads_d, w_out, gain_mlp, w_up, w_down, y_ref, mixed, None, None)


def wrap(index, count):
    return lax.rem(index + count, count)


class Stream:
    def __init__(self, axis, sent, heads, got, outs, keys, vals, queries, board, tops, sems):
        self.axis, self.sent, self.heads, self.got, self.outs = axis, sent, heads, got, outs
        self.keys, self.vals, self.queries, self.board, self.tops = keys, vals, queries, board, tops
        self.send_in, self.recv_in, self.send_out, self.recv_out, self.local = sems
        self.count, self.items, _, self.width = got.shape
        self.me = lax.axis_index(axis)
        self.units = self.count * self.items

    def greet(self, barrier):
        for step in range(1, self.count):
            pl.semaphore_signal(barrier, inc=1, device_id={self.axis: wrap(self.me + step, self.count)})

    def inward(self, item, step):
        target = wrap(self.me + step, self.count)
        return pltpu.make_async_remote_copy(
            src_ref=self.sent.at[target, item],
            dst_ref=self.got.at[step, item],
            send_sem=self.send_in.at[item, step],
            recv_sem=self.recv_in.at[item, step],
            device_id={self.axis: target},
        )

    def outward(self, item, step):
        return pltpu.make_async_remote_copy(
            src_ref=self.outs.at[step, item],
            dst_ref=self.heads.at[self.me, item],
            send_sem=self.send_out.at[item, step],
            recv_sem=self.recv_out.at[item, step],
            device_id={self.axis: wrap(self.me - step, self.count)},
        )

    def own(self):
        return pltpu.make_async_copy(self.sent.at[self.me], self.got.at[0], self.local)

    def start(self, item):
        for step in range(1, self.count):
            self.inward(item, step).start()

    def prepare(self, item):
        for step in range(1, self.count):
            self.inward(item, step).wait_recv()
        slot = lax.rem(item, 2)
        for src in range(self.count):
            q = self.got[src, item, :HD].astype(jnp.float32) * SCALE
            high = q.astype(jnp.bfloat16)
            low = (q - high.astype(jnp.float32)).astype(jnp.bfloat16)
            self.queries[slot, src] = jnp.concatenate([high, low], axis=0)
            k = self.got[src, item, HD : 2 * HD]
            self.keys[slot, src * self.width : (src + 1) * self.width] = jnp.concatenate([k, k], axis=0).T
            self.vals[slot, src] = self.got[src, item, 2 * HD :]

    def step(self, after, unit):
        count, width = self.count, self.width
        if after is not None:
            after, odd = after
            fresh = lax.rem(after // count, 2)
            q = self.queries[fresh, lax.rem(after, count)]
            tops = []
        if unit is not None:
            unit, even = unit
            item, block = unit // count, lax.rem(unit, count)
            slot = lax.rem(item, 2)
            top = self.tops[even][...]
            sums, total = 0.0, 0.0
        for src in range(count):
            here = slice(src * width, (src + 1) * width)
            if after is not None:
                scores = jnp.dot(self.keys[fresh, here], q, preferred_element_type=jnp.float32)
                self.board[odd][here] = scores
                tops.append(jnp.max(scores.reshape(-1, 8, width), axis=0))
            if unit is not None:
                probs = jnp.exp2(self.board[even][here] - top)
                sums += jnp.sum(probs.reshape(-1, 8, width), axis=0)
                total += jnp.dot(
                    self.vals[slot, src], probs.astype(jnp.bfloat16), preferred_element_type=jnp.float32
                )
        if after is not None:
            self.tops[odd][...] = jnp.max(functools.reduce(jnp.maximum, tops), axis=0, keepdims=True)
        if unit is not None:
            self.outs[block, item] = (total / jnp.sum(sums, axis=0, keepdims=True)).astype(jnp.bfloat16)

    def deliver(self, unit):
        item, block = unit // self.count, lax.rem(unit, self.count)

        @pl.when(block == 0)
        def _():
            self.heads[self.me, item] = self.outs[0, item]

        @pl.when(block != 0)
        def _():
            self.outward(item, block).start()

    def run(self):
        unroll = UNROLL
        assert self.count % unroll == 0
        self.prepare(0)
        for ahead in range(LAG):
            self.step((ahead, ahead), None)

        @pl.loop(0, self.units, step=unroll)
        def _(unit):
            after = unit + unroll

            @pl.when(jnp.logical_and(lax.rem(after, self.count) == 0, after < self.units))
            def _():
                self.prepare(after // self.count)

            for ahead in range(unroll):
                self.step((unit + ahead + LAG, (ahead + LAG) % unroll), (unit + ahead, ahead))

            @pl.when(unit > 0)
            def _():
                self.deliver(unit - 1)

            for ahead in range(unroll - 1):
                self.deliver(unit + ahead)

        self.deliver(self.units - 1)

    def drain(self):
        for item in range(self.items):
            for step in range(1, self.count):
                self.inward(item, step).wait_send()
                self.outward(item, step).wait()


def layer_kernel(
    sent_a, sent_d, heads_a, heads_d, got_a, got_d, outs_a, outs_d, keys, vals, queries, *rest
):
    boards, tops, sems = rest[:UNROLL], rest[UNROLL : 2 * UNROLL], rest[2 * UNROLL :]

    def stream(axis, sent, heads, got, outs, sems):
        count, _, _, width = got.shape
        return Stream(
            axis,
            sent,
            heads,
            got,
            outs,
            keys.at[:, : count * width],
            vals.at[:, :count],
            queries.at[:, :count],
            [board.at[: count * width] for board in boards],
            tops,
            sems,
        )

    across = stream("col", sent_a, heads_a, got_a, outs_a, sems[:5])
    down = stream("row", sent_d, heads_d, got_d, outs_d, sems[5:])
    barrier = pltpu.get_barrier_semaphore()
    across.greet(barrier)
    down.greet(barrier)
    pl.semaphore_wait(barrier, across.count + down.count - 2)
    for item in range(down.items):
        down.start(item)
        if item == 0:
            across.start(item)
    for item in range(1, across.items):
        across.start(item)
    across.own().start()
    down.own().start()
    across.own().wait()
    down.own().wait()
    down.run()
    across.run()
    down.drain()
    across.drain()


VM = pl.BlockSpec(memory_space=pltpu.VMEM)


def call(kernel, outs, scratch, *args, params=None):
    def spec(arg):
        if not isinstance(arg, tuple):
            return VM
        array, layer = arg
        rest = array.shape[1:]
        return pl.BlockSpec((None,) + rest, lambda i: (layer,) + (0,) * len(rest))

    return pl.pallas_call(
        kernel,
        out_shape=outs,
        grid=(1,),
        in_specs=[spec(arg) for arg in args],
        out_specs=jax.tree.map(lambda _: VM, outs),
        scratch_shapes=scratch,
        compiler_params=params,
    )(*[arg[0] if isinstance(arg, tuple) else arg for arg in args])


def split(array, axis):
    return array.reshape(lax.axis_size(axis), -1, *array.shape[-2:])


def attend(sent_a, sent_d, layer):
    sent_a, sent_d = split(sent_a, "col"), split(sent_d, "row")
    scratch, sems, outs = [], [], []
    for sent in (sent_a, sent_d):
        count, items, _, width = sent.shape
        outs.append(jax.ShapeDtypeStruct((count, items, HD, width), jnp.bfloat16))
        scratch.append(pltpu.VMEM(sent.shape, jnp.bfloat16))
        sems += [pltpu.SemaphoreType.DMA((items, count))] * 4 + [pltpu.SemaphoreType.DMA]
    for out in outs:
        scratch.append(pltpu.VMEM(out.shape, jnp.bfloat16))
    count = max(sent_a.shape[0], sent_d.shape[0])
    width = max(sent_a.shape[-1], sent_d.shape[-1])
    scratch += [
        pltpu.VMEM((2, count * width, 2 * HD), jnp.bfloat16),
        pltpu.VMEM((2, count, HD, width), jnp.bfloat16),
        pltpu.VMEM((2, count, 2 * HD, width), jnp.bfloat16),
    ]
    scratch += [pltpu.VMEM((count * width, width), jnp.float32)] * UNROLL
    scratch += [pltpu.VMEM((1, width), jnp.float32)] * UNROLL
    heads = call(
        layer_kernel,
        tuple(outs),
        scratch + sems,
        sent_a,
        sent_d,
        params=pltpu.CompilerParams(collective_id=layer, has_side_effects=True),
    )
    return [array.reshape(-1, *array.shape[-2:]) for array in heads]


def shards(frame, gain_attn, w_qkv, w_out, gain_mlp, w_up, w_down):
    rows, cols, _ = frame.shape
    items_a = rows // SW * HALF
    items_d = cols // SW * HALF
    sent = (
        jax.ShapeDtypeStruct((items_a, 3 * HD, SW * cols), jnp.bfloat16),
        jax.ShapeDtypeStruct((items_d, 3 * HD, SW * rows), jnp.bfloat16),
    )
    tokens = pltpu.VMEM((rows, cols // SW, SW, D), jnp.float32)
    flipped = pltpu.VMEM((3, D, D), jnp.bfloat16)
    shape = jax.ShapeDtypeStruct(frame.shape, jnp.bfloat16)
    state = frame
    sent_a, sent_d = call(functools.partial(first_kernel, 0), sent, [tokens, flipped], frame, gain_attn, (w_qkv, 0))
    for layer in range(LAYERS):
        heads_a, heads_d = attend(sent_a, sent_d, layer)
        args = (state, heads_a, heads_d, (w_out, layer), gain_mlp, (w_up, layer), (w_down, layer))
        if layer + 1 < LAYERS:
            state, sent_a, sent_d = call(
                functools.partial(middle_kernel, layer),
                (shape,) + sent,
                [tokens, tokens, flipped],
                *args,
                gain_attn,
                (w_qkv, layer + 1),
            )
        else:
            state = call(functools.partial(last_kernel, layer), shape, [tokens], *args)
    return state


def solution(mesh):
    placed = (P("row", "col", None), P(), P(), P(), P(), P(), P())
    return jax.shard_map(
        shards, mesh=mesh, in_specs=placed, out_specs=P("row", "col", None), check_vma=False
    )
```

```python
import functools
import math

import jax
import jax.numpy as jnp
from jax import lax
from jax.experimental import pallas as pl
from jax.experimental.pallas import tpu as pltpu
from jax.sharding import PartitionSpec as P

D = 256
HEADS = 8
SW = 8
LAYERS = 2
HALF = HEADS // 2
HD = D // HEADS
EPS = 1e-05
UNROLL = 4
LAG = 2
SCALE = HD**-0.5 * math.log2(math.e)


def normalize(floats, gain):
    center = floats - jnp.mean(floats, axis=-1, keepdims=True)
    spread = jnp.mean(center * center, axis=-1, keepdims=True)
    return center * lax.rsqrt(spread + EPS) * gain


def project(normed, w_ref, sent_a, sent_d, wt):
    rows, bands, _, _ = normed.shape
    side = HALF * HD
    for part in range(3):
        wt[part] = w_ref[:, part * D : (part + 1) * D].T

    def emit(tokens, first, sent, band):
        tokens = tokens.reshape(-1, D).astype(jnp.bfloat16)
        for part in range(3):
            out = lax.dot_general(
                wt[part, first : first + side],
                tokens,
                (((1,), (1,)), ((), ())),
                preferred_element_type=jnp.float32,
            )
            sent[band * HALF : (band + 1) * HALF, part * HD : (part + 1) * HD] = (
                out.astype(jnp.bfloat16).reshape(HALF, HD, -1)
            )

    for band in range(bands):
        emit(normed[:, band], side, sent_d, band)
    for band in range(rows // SW):
        emit(normed[band * SW : (band + 1) * SW], 0, sent_a, band)


def first_kernel(layer, x_ref, gain_ref, w_ref, sent_a, sent_d, normed, wt):
    rows, cols, _ = x_ref.shape
    for band in range(rows // SW):
        part = slice(band * SW, (band + 1) * SW)
        floats = x_ref[part].reshape(-1, D).astype(jnp.float32)
        normed[part] = normalize(floats, gain_ref[layer : layer + 1]).reshape(SW, cols // SW, SW, D)
    project(normed, w_ref, sent_a, sent_d, wt)


def rest(layer, x_ref, heads_a, heads_d, w_out, gain_mlp, w_up, w_down, y_ref, mixed, normed, gain):
    rows, cols, _ = x_ref.shape
    bands = cols // SW
    flip = (((0,), (0,)), ((), ()))
    for band in range(bands):
        heads = heads_d[band * HALF : (band + 1) * HALF].reshape(HALF * HD, -1)
        part = lax.dot_general(heads, w_out[HALF * HD :], flip, preferred_element_type=jnp.float32)
        mixed[:, band] = part.reshape(rows, SW, D)
    for band in range(rows // SW):
        here = slice(band * SW, (band + 1) * SW)
        heads = heads_a[band * HALF : (band + 1) * HALF].reshape(HALF * HD, -1)
        part = lax.dot_general(heads, w_out[: HALF * HD], flip, preferred_element_type=jnp.float32)
        total = x_ref[here].reshape(-1, D).astype(jnp.float32) + (part + mixed[here].reshape(-1, D))
        normed2 = normalize(total, gain_mlp[layer : layer + 1]).astype(jnp.bfloat16)
        up = jnp.dot(normed2, w_up[...], preferred_element_type=jnp.float32)
        hidden = jax.nn.gelu(up, approximate=True).astype(jnp.bfloat16)
        final = total + jnp.dot(hidden, w_down[...], preferred_element_type=jnp.float32)
        final = final.astype(jnp.bfloat16)
        y_ref[here] = final.reshape(SW, cols, D)
        if normed is not None:
            normed[here] = normalize(final.astype(jnp.float32), gain[layer + 1 : layer + 2]).reshape(SW, bands, SW, D)


def middle_kernel(
    layer, x_ref, heads_a, heads_d, w_out, gain_mlp, w_up, w_down, gain, w_ref, y_ref, sent_a, sent_d, mixed, normed, wt
):
    rest(layer, x_ref, heads_a, heads_d, w_out, gain_mlp, w_up, w_down, y_ref, mixed, normed, gain)
    project(normed, w_ref, sent_a, sent_d, wt)


def last_kernel(layer, x_ref, heads_a, heads_d, w_out, gain_mlp, w_up, w_down, y_ref, mixed):
    rest(layer, x_ref, heads_a, heads_d, w_out, gain_mlp, w_up, w_down, y_ref, mixed, None, None)


def wrap(index, count):
    return lax.rem(index + count, count)


class Stream:
    def __init__(self, axis, sent, heads, got, outs, keys, vals, queries, board, tops, sems):
        self.axis, self.sent, self.heads, self.got, self.outs = axis, sent, heads, got, outs
        self.keys, self.vals, self.queries, self.board, self.tops = keys, vals, queries, board, tops
        self.send_in, self.recv_in, self.send_out, self.recv_out, self.local = sems
        self.count, self.items, _, self.width = got.shape
        self.me = lax.axis_index(axis)
        self.units = self.count * self.items

    def greet(self, barrier):
        for step in range(1, self.count):
            pl.semaphore_signal(barrier, inc=1, device_id={self.axis: wrap(self.me + step, self.count)})

    def inward(self, item, step):
        target = wrap(self.me + step, self.count)
        return pltpu.make_async_remote_copy(
            src_ref=self.sent.at[target, item],
            dst_ref=self.got.at[step, item],
            send_sem=self.send_in.at[item, step],
            recv_sem=self.recv_in.at[item, step],
            device_id={self.axis: target},
        )

    def outward(self, item, step):
        return pltpu.make_async_remote_copy(
            src_ref=self.outs.at[step, item],
            dst_ref=self.heads.at[self.me, item],
            send_sem=self.send_out.at[item, step],
            recv_sem=self.recv_out.at[item, step],
            device_id={self.axis: wrap(self.me - step, self.count)},
        )

    def own(self):
        return pltpu.make_async_copy(self.sent.at[self.me], self.got.at[0], self.local)

    def start(self, item):
        for step in range(1, self.count):
            self.inward(item, step).start()

    def prepare(self, item):
        for step in range(1, self.count):
            self.inward(item, step).wait_recv()
        slot = lax.rem(item, 2)
        for src in range(self.count):
            q = self.got[src, item, :HD].astype(jnp.float32) * SCALE
            high = q.astype(jnp.bfloat16)
            low = (q - high.astype(jnp.float32)).astype(jnp.bfloat16)
            self.queries[slot, src] = jnp.concatenate([high, low], axis=0)
            k = self.got[src, item, HD : 2 * HD]
            self.keys[slot, src * self.width : (src + 1) * self.width] = jnp.concatenate([k, k], axis=0).T
            self.vals[slot, src] = self.got[src, item, 2 * HD :]

    def step(self, after, unit):
        count, width = self.count, self.width
        if after is not None:
            after, odd = after
            fresh = lax.rem(after // count, 2)
            q = self.queries[fresh, lax.rem(after, count)]
            tops = []
        if unit is not None:
            unit, even = unit
            item, block = unit // count, lax.rem(unit, count)
            slot = lax.rem(item, 2)
            top = self.tops[even][...]
            sums, total = 0.0, 0.0
        for src in range(count):
            here = slice(src * width, (src + 1) * width)
            if after is not None:
                scores = jnp.dot(self.keys[fresh, here], q, preferred_element_type=jnp.float32)
                self.board[odd][here] = scores
                tops.append(jnp.max(scores.reshape(-1, 8, width), axis=0))
            if unit is not None:
                probs = jnp.exp2(self.board[even][here] - top)
                sums += jnp.sum(probs.reshape(-1, 8, width), axis=0)
                total += jnp.dot(
                    self.vals[slot, src], probs.astype(jnp.bfloat16), preferred_element_type=jnp.float32
                )
        if after is not None:
            self.tops[odd][...] = jnp.max(functools.reduce(jnp.maximum, tops), axis=0, keepdims=True)
        if unit is not None:
            self.outs[block, item] = (total / jnp.sum(sums, axis=0, keepdims=True)).astype(jnp.bfloat16)

    def deliver(self, unit):
        item, block = unit // self.count, lax.rem(unit, self.count)

        @pl.when(block == 0)
        def _():
            self.heads[self.me, item] = self.outs[0, item]

        @pl.when(block != 0)
        def _():
            self.outward(item, block).start()

    def run(self):
        unroll = UNROLL
        assert self.count % unroll == 0
        self.prepare(0)
        for ahead in range(LAG):
            self.step((ahead, ahead), None)

        @pl.loop(0, self.units, step=unroll)
        def _(unit):
            after = unit + unroll

            @pl.when(jnp.logical_and(lax.rem(after, self.count) == 0, after < self.units))
            def _():
                self.prepare(after // self.count)

            @pl.when(unit > 0)
            def _():
                self.outward((unit - 1) // self.count, lax.rem(unit - 1, self.count)).start()

            item, block = unit // self.count, lax.rem(unit, self.count)
            for ahead in range(unroll):
                self.step((unit + ahead + LAG, (ahead + LAG) % unroll), (unit + ahead, ahead))
                if ahead > 1:
                    self.outward(item, block + ahead - 1).start()
            self.deliver(unit)

        self.deliver(self.units - 1)

    def drain(self):
        for item in range(self.items):
            for step in range(1, self.count):
                self.inward(item, step).wait_send()
                self.outward(item, step).wait()


def layer_kernel(
    sent_a, sent_d, heads_a, heads_d, got_a, got_d, outs_a, outs_d, keys, vals, queries, *rest
):
    boards, tops, sems = rest[:UNROLL], rest[UNROLL : 2 * UNROLL], rest[2 * UNROLL :]

    def stream(axis, sent, heads, got, outs, sems):
        count, _, _, width = got.shape
        return Stream(
            axis,
            sent,
            heads,
            got,
            outs,
            keys.at[:, : count * width],
            vals.at[:, :count],
            queries.at[:, :count],
            [board.at[: count * width] for board in boards],
            tops,
            sems,
        )

    across = stream("col", sent_a, heads_a, got_a, outs_a, sems[:5])
    down = stream("row", sent_d, heads_d, got_d, outs_d, sems[5:])
    barrier = pltpu.get_barrier_semaphore()
    across.greet(barrier)
    down.greet(barrier)
    pl.semaphore_wait(barrier, across.count + down.count - 2)
    for item in range(down.items):
        down.start(item)
        if item == 0:
            across.start(item)
    for item in range(1, across.items):
        across.start(item)
    across.own().start()
    down.own().start()
    across.own().wait()
    down.own().wait()
    down.run()
    across.run()
    down.drain()
    across.drain()


VM = pl.BlockSpec(memory_space=pltpu.VMEM)


def call(kernel, outs, scratch, *args, params=None):
    def spec(arg):
        if not isinstance(arg, tuple):
            return VM
        array, layer = arg
        rest = array.shape[1:]
        return pl.BlockSpec((None,) + rest, lambda i: (layer,) + (0,) * len(rest))

    return pl.pallas_call(
        kernel,
        out_shape=outs,
        grid=(1,),
        in_specs=[spec(arg) for arg in args],
        out_specs=jax.tree.map(lambda _: VM, outs),
        scratch_shapes=scratch,
        compiler_params=params,
    )(*[arg[0] if isinstance(arg, tuple) else arg for arg in args])


def split(array, axis):
    return array.reshape(lax.axis_size(axis), -1, *array.shape[-2:])


def attend(sent_a, sent_d, layer):
    sent_a, sent_d = split(sent_a, "col"), split(sent_d, "row")
    scratch, sems, outs = [], [], []
    for sent in (sent_a, sent_d):
        count, items, _, width = sent.shape
        outs.append(jax.ShapeDtypeStruct((count, items, HD, width), jnp.bfloat16))
        scratch.append(pltpu.VMEM(sent.shape, jnp.bfloat16))
        sems += [pltpu.SemaphoreType.DMA((items, count))] * 4 + [pltpu.SemaphoreType.DMA]
    for out in outs:
        scratch.append(pltpu.VMEM(out.shape, jnp.bfloat16))
    count = max(sent_a.shape[0], sent_d.shape[0])
    width = max(sent_a.shape[-1], sent_d.shape[-1])
    scratch += [
        pltpu.VMEM((2, count * width, 2 * HD), jnp.bfloat16),
        pltpu.VMEM((2, count, HD, width), jnp.bfloat16),
        pltpu.VMEM((2, count, 2 * HD, width), jnp.bfloat16),
    ]
    scratch += [pltpu.VMEM((count * width, width), jnp.float32)] * UNROLL
    scratch += [pltpu.VMEM((1, width), jnp.float32)] * UNROLL
    heads = call(
        layer_kernel,
        tuple(outs),
        scratch + sems,
        sent_a,
        sent_d,
        params=pltpu.CompilerParams(collective_id=layer, has_side_effects=True),
    )
    return [array.reshape(-1, *array.shape[-2:]) for array in heads]


def shards(frame, gain_attn, w_qkv, w_out, gain_mlp, w_up, w_down):
    rows, cols, _ = frame.shape
    items_a = rows // SW * HALF
    items_d = cols // SW * HALF
    sent = (
        jax.ShapeDtypeStruct((items_a, 3 * HD, SW * cols), jnp.bfloat16),
        jax.ShapeDtypeStruct((items_d, 3 * HD, SW * rows), jnp.bfloat16),
    )
    tokens = pltpu.VMEM((rows, cols // SW, SW, D), jnp.float32)
    flipped = pltpu.VMEM((3, D, D), jnp.bfloat16)
    shape = jax.ShapeDtypeStruct(frame.shape, jnp.bfloat16)
    state = frame
    sent_a, sent_d = call(functools.partial(first_kernel, 0), sent, [tokens, flipped], frame, gain_attn, (w_qkv, 0))
    for layer in range(LAYERS):
        heads_a, heads_d = attend(sent_a, sent_d, layer)
        args = (state, heads_a, heads_d, (w_out, layer), gain_mlp, (w_up, layer), (w_down, layer))
        if layer + 1 < LAYERS:
            state, sent_a, sent_d = call(
                functools.partial(middle_kernel, layer),
                (shape,) + sent,
                [tokens, tokens, flipped],
                *args,
                gain_attn,
                (w_qkv, layer + 1),
            )
        else:
            state = call(functools.partial(last_kernel, layer), shape, [tokens], *args)
    return state


def solution(mesh):
    placed = (P("row", "col", None), P(), P(), P(), P(), P(), P())
    return jax.shard_map(
        shards, mesh=mesh, in_specs=placed, out_specs=P("row", "col", None), check_vma=False
    )
```
